32 devices in a mesh: group: 2 (over x), ctx: 16 (over z, y, core).
Axes of the slice: x: 2, y: 2, z: 4, core: 2. Of those that a mesh axis runs over, the one named last changes fastest.
Arguments:
- query_proj: bfloat16 [8192, 2048], P(('group', 'ctx')), parts along dimension 0, may hold values from -6 to 6
- key_proj: bfloat16 [8192, 2048], P(('group', 'ctx')), parts along dimension 0, may hold values from -6 to 6
- value_proj: bfloat16 [8192, 2048], P(('group', 'ctx')), parts along dimension 0, may hold values from -6 to 6
- short_weight: float32 [3, 3, 2048], replicated, may hold values from -3.5 to 3.5
- decay_rate: float32 [16, 2048], replicated, may hold values from 4.8828125e-05 to 0.125
- residue: float32 [16, 2048], replicated, may hold values from -0.5 to 0.5
- skip_gain: float32 [2048], replicated, may hold values from -4 to 4
Outputs:
- mixed: bfloat16 [8192, 2048], P(('group', 'ctx')), parts along dimension 0
The draws below stay inside these ranges and needn't reach their ends.
There are 2 independent parts, one for each index of `group`. The reference program is written for one: setup_inputs(seed, part) draws one part's arguments, and reference() takes and returns one part's arrays. A program takes and returns all parts, laid end to end along the dimension named above; an argument that names none is the same for every part. Nothing has to cross between parts.
All inputs are finite; a program needn't handle non-finite values.
Results may differ from the reference program's by a relative error of at most 0.001.
Values may be sent and summed in bfloat16 or wider, within the bound.
A program may use at most 128 MiB of HBM per device.

```python
import math
import jax
import jax.numpy as jnp
from jax import lax

C = 2048
ORDER = 16
SHORT = 3
SEQ = 4096


def modal_pair(key):
    base = jax.random.fold_in(key, 1301)
    flag_key = jax.random.fold_in(base, 1)
    rate_key = jax.random.fold_in(base, 2)
    weight_key = jax.random.fold_in(base, 3)
    fast_key = jax.random.fold_in(base, 4)
    slow_flag = jax.random.randint(flag_key, (1, C), 0, 2)
    slow_rate = jnp.exp(jax.random.uniform(rate_key, (ORDER, C), jnp.float32, math.log(0.3 / SEQ), math.log(2.0 / SEQ)))
    fast_rate = jnp.exp(jax.random.uniform(fast_key, (ORDER, C), jnp.float32, math.log(1.0 / 50.0), math.log(0.125)))
    rate = jnp.where(slow_flag == 1, slow_rate, fast_rate)
    normed = jax.random.truncated_normal(weight_key, -4.0, 4.0, (ORDER, C), jnp.float32)
    weight = normed * jnp.sqrt(2.0 * rate / ORDER)
    return (rate, weight)


def draw_decay_rate(key, part):
    rate, weight = modal_pair(key)
    return rate


def draw_residue(key, part):
    rate, weight = modal_pair(key)
    return weight


def block_scale(own_key, extent, cuts, least, largest):
    level = 1.0
    for axis_at, parts in cuts:
        heights = jax.random.uniform(jax.random.fold_in(jax.random.fold_in(own_key, 6), axis_at), (parts,), jnp.float32, least / len(cuts), largest / len(cuts))
        level = level * jnp.repeat(jnp.exp(heights), extent[axis_at] // parts).reshape((-1,) + (1,) * (len(extent) - 1 - axis_at))
    return level


def noise(key, shape, deviation, bound, cuts=(), dtype=jnp.bfloat16):
    values = deviation * jax.random.normal(key, shape, jnp.float32)
    if cuts:
        values = values * block_scale(key, shape, cuts, -0.22, 0.18)
    return jnp.clip(values, -bound, bound).astype(dtype)


def setup_inputs(seed: int = 0, part: int = 0) -> dict:
    key_list = jax.random.split(jax.random.key(seed), 8)
    part_keys = jax.random.split(jax.random.fold_in(key_list[7], part), 8)
    return {
        "query_proj": noise(part_keys[0], (SEQ, C), 1.0, 6.0, ((0, 16),)),
        "key_proj": noise(part_keys[1], (SEQ, C), 1.0, 6.0, ((0, 16),)),
        "value_proj": noise(part_keys[2], (SEQ, C), 1.0, 6.0, ((0, 16),)),
        "short_weight": noise(key_list[3], (3, SHORT, C), SHORT ** -0.5, 3.5, (), jnp.float32),
        "decay_rate": draw_decay_rate(jax.random.fold_in(key_list[7], 71), part),
        "residue": draw_residue(jax.random.fold_in(key_list[7], 71), part),
        "skip_gain": noise(key_list[6], (C,), 1.0, 4.0, (), jnp.float32),
    }


def causal_short(rows, weights):
    taps = weights.shape[0]
    length = rows.shape[0]
    padding = jnp.zeros((taps - 1, rows.shape[1]), jnp.float32)
    extended = jnp.concatenate([padding, rows.astype(jnp.float32)], axis=0)
    total = weights[0] * extended[taps - 1:]
    for lag in range(1, taps):
        total = total + weights[lag] * extended[taps - 1 - lag: taps - 1 - lag + length]
    return total


def reference(query_proj, key_proj, value_proj, short_weight, decay_rate, residue, skip_gain):
    query_conv = causal_short(query_proj, short_weight[0])
    key_conv = causal_short(key_proj, short_weight[1])
    value_conv = causal_short(value_proj, short_weight[2])
    gated = key_conv * value_conv
    times = jnp.arange(SEQ).astype(jnp.float32)

    def add_mode(total, pair):
        rate, weight = pair
        return total + weight * jnp.exp(-rate * times[:, None]), None

    response, unused = lax.scan(add_mode, jnp.zeros((SEQ, C), jnp.float32), (decay_rate, residue))
    spectra = jnp.fft.rfft(gated, n=2 * SEQ, axis=0) * jnp.fft.rfft(response, n=2 * SEQ, axis=0)
    conv = jnp.fft.irfft(spectra, n=2 * SEQ, axis=0)[:SEQ]
    return (query_conv * (conv + skip_gain * gated)).astype(jnp.bfloat16)
```

```python
import functools

import jax
import jax.numpy as jnp
from jax import lax
from jax.experimental import pallas as pl
from jax.experimental.pallas import tpu as pltpu
from jax.sharding import PartitionSpec as P

MESH = pl.DeviceIdType.MESH
F32 = jnp.float32
BF16 = jnp.bfloat16
LANES = 128
SUBS = 8


def tree_sum(x):
    while x.shape[0] > 1:
        half = x.shape[0] // 2
        x = x[:half] + x[half:]
    return x[0]


def layer_kernel(
    parts, q_hbm, k_hbm, v_hbm, sw_hbm, rate_hbm, res_hbm, skip_hbm, out_hbm,
    qbuf, kbuf, vbuf, tail16, sw, rate, res, skip,
    perm, qx, kx, vx, tail, halo,
    a1, a32, a64, a128, a256, resp, g_s, y_s, x_s, w_s, z_s, qc_s,
    ends, got, back, inc, obuf,
    tail_sem, load_sem, par_sem, halo_sem, send_a, recv_a, send_b, recv_b, out_sem,
):
    tokens, channels = qbuf.shape
    modes = rate.shape[0]
    groups = channels // LANES
    steps = tokens // SUBS
    units = groups * modes // SUBS
    own = units // parts
    per_group = modes // SUBS // own
    me = lax.axis_index("ctx")
    barrier = pltpu.get_barrier_semaphore()

    tail_copies = []
    for i, src in enumerate((k_hbm, v_hbm, q_hbm)):
        c = pltpu.make_async_copy(src.at[pl.ds(tokens - 16, 16)], tail16.at[i], tail_sem.at[i])
        c.start()
        tail_copies.append(c)
    par_copies = []
    for i, (src, dst) in enumerate(((rate_hbm, rate), (res_hbm, res), (sw_hbm, sw), (skip_hbm, skip))):
        c = pltpu.make_async_copy(src, dst, par_sem.at[i])
        c.start()
        par_copies.append(c)
    loads = []
    for i, (src, dst) in enumerate(((k_hbm, kbuf), (v_hbm, vbuf), (q_hbm, qbuf))):
        c = pltpu.make_async_copy(src, dst, load_sem.at[i])
        c.start()
        loads.append(c)

    halo[...] = jnp.zeros(halo.shape, F32)

    def greet(i, carry):
        peer = lax.rem(me + i, parts)
        pl.semaphore_signal(barrier, inc=1, device_id={"ctx": peer}, device_id_type=MESH)
        return carry

    lax.fori_loop(1, parts, greet, 0)

    tail[...] = jnp.zeros(tail.shape, F32)
    for i in range(3):
        tail_copies[i].wait()
        tail[2 * i : 2 * i + 2, :] = tail16[i].astype(F32)[14:16, :]
    pl.semaphore_wait(barrier, parts - 1)

    halo_copy = pltpu.make_async_remote_copy(
        src_ref=tail, dst_ref=halo, send_sem=halo_sem.at[0], recv_sem=halo_sem.at[1],
        device_id={"ctx": lax.rem(me + 1, parts)}, device_id_type=MESH,
    )

    @pl.when(me < parts - 1)
    def _():
        halo_copy.start()

    for c in par_copies:
        c.wait()
    negative = -rate[...]
    a1[...] = jnp.exp(negative)
    a32[...] = jnp.exp(negative * steps)
    a64[...] = jnp.exp(negative * (2 * steps))
    a128[...] = jnp.exp(negative * (4 * steps))
    for u in range(units):
        col = (u * SUBS // modes) * LANES
        row = (u * SUBS) % modes
        a256[u] = jnp.exp(rate[row : row + SUBS, col : col + LANES] * (-float(tokens)))

    row_id = lax.broadcasted_iota(jnp.int32, (tokens, tokens), 0)
    col_id = lax.broadcasted_iota(jnp.int32, (tokens, tokens), 1)
    perm[0] = jnp.where(col_id == (row_id % SUBS) * steps + row_id // SUBS, 1.0, 0.0).astype(BF16)
    perm[1] = jnp.where(row_id == (col_id % SUBS) * steps + col_id // SUBS, 1.0, 0.0).astype(BF16)

    sub_f = lax.broadcasted_iota(jnp.int32, (SUBS, LANES), 0).astype(F32)
    sub_w = lax.broadcasted_iota(jnp.int32, (SUBS, channels), 0)
    sub_m = lax.broadcasted_iota(jnp.int32, (modes, SUBS, LANES), 1)

    def lanes_of(cg):
        return pl.ds(pl.multiple_of(cg * LANES, LANES), LANES)

    def spread(ref, lanes):
        return jnp.stack([jnp.broadcast_to(ref[n : n + 1, lanes], (SUBS, LANES)) for n in range(modes)])

    def response(cg, carry):
        lanes = lanes_of(cg)
        rates = spread(rate, lanes)
        wave = spread(res, lanes) * jnp.exp(rates * (-sub_f)[None])
        eight = jnp.exp(rates * (-float(SUBS)))
        for b in range(steps // SUBS):
            resp[cg, SUBS * b : SUBS * b + SUBS, :] = tree_sum(wave)
            if b + 1 < steps // SUBS:
                wave = wave * eight
        return carry

    lax.fori_loop(0, groups, response, 0)

    def permuted(buf, dst):
        for c in range(0, channels, 256):
            dst[2 * SUBS :, c : c + 256] = jnp.dot(
                perm[0], buf[:, c : c + 256], preferred_element_type=F32
            )

    def margin(dst, row):
        for lag in (1, 2):
            last = dst[2 * SUBS + tokens - SUBS * lag : 2 * SUBS + tokens - SUBS * (lag - 1), :]
            before = jnp.broadcast_to(halo[row + 2 - lag : row + 3 - lag, :], (SUBS, channels))
            dst[2 * SUBS - SUBS * lag : 2 * SUBS - SUBS * (lag - 1), :] = jnp.where(
                sub_w == 0, before, pltpu.roll(last, 1, 0)
            )

    loads[0].wait()
    permuted(kbuf, kx)
    loads[1].wait()
    permuted(vbuf, vx)

    @pl.when(me > 0)
    def _():
        halo_copy.wait_recv()

    margin(kx, 0)
    margin(vx, 2)

    def rows(j):
        return slice(SUBS * j, SUBS * j + SUBS)

    def tap(stream, lag, lanes):
        return jnp.broadcast_to(sw[stream, lag : lag + 1, lanes], (SUBS, LANES))

    def send_ends(owner):
        return pltpu.make_async_remote_copy(
            src_ref=ends.at[pl.ds(owner * own, own)], dst_ref=got.at[me],
            send_sem=send_a.at[owner], recv_sem=recv_a.at[me],
            device_id={"ctx": owner}, device_id_type=MESH,
        )

    def states(i, carry):
        cg = lax.rem(me * own // (modes // SUBS) + i, groups)
        lanes = lanes_of(cg)
        a = spread(a1, lanes)
        wk = [tap(1, lag, lanes) for lag in range(3)]
        wv = [tap(2, lag, lanes) for lag in range(3)]
        k2, k1 = kx[rows(0), lanes], kx[rows(1), lanes]
        v2, v1 = vx[rows(0), lanes], vx[rows(1), lanes]
        h = None
        for j in range(steps):
            k0, v0 = kx[rows(j + 2), lanes], vx[rows(j + 2), lanes]
            g = (wk[0] * k0 + wk[1] * k1 + wk[2] * k2) * (wv[0] * v0 + wv[1] * v1 + wv[2] * v2)
            k2, k1, v2, v1 = k1, k0, v1, v0
            g_s[cg, rows(j), :] = g
            h = jnp.broadcast_to(g[None], (modes, SUBS, LANES)) if h is None else a * h + g[None]
        for lag, ref in ((1, a32), (2, a64), (4, a128)):
            factor = jnp.where(sub_m >= lag, spread(ref, lanes), 0.0)
            h = h + factor * pltpu.roll(h, lag, 1)
        x_s[cg] = h
        for n in range(modes):
            ends[cg * (modes // SUBS) + n // SUBS, n % SUBS : n % SUBS + 1, :] = h[n, SUBS - 1 : SUBS, :]
        for p in range(per_group):
            owner = cg * per_group + p

            @pl.when(owner != me)
            def _():
                send_ends(owner).start()

            @pl.when(owner == me)
            def _():
                got[me] = ends[pl.ds(owner * own, own)]

        return carry

    lax.fori_loop(0, groups, states, 0)

    loads[2].wait()
    permuted(qbuf, qx)
    margin(qx, 4)

    def local(cg, carry):
        lanes = lanes_of(cg)
        gain = jnp.broadcast_to(skip[0:1, lanes], (SUBS, LANES))
        wq = [tap(0, lag, lanes) for lag in range(3)]
        for jb in range(steps // SUBS):
            acc = [None] * SUBS
            for ib in range(jb + 1):
                gs = [g_s[cg, rows(ib * SUBS + i), :] for i in range(SUBS)]
                base = SUBS * (jb - ib)
                taps = {
                    d: jnp.broadcast_to(resp[cg, base + d : base + d + 1, :], (SUBS, LANES))
                    for d in range(1 - SUBS, SUBS)
                    if base + d >= 0
                }
                for i in range(SUBS):
                    for j in range(SUBS):
                        if j - i in taps:
                            term = taps[j - i] * gs[i]
                            acc[j] = term if acc[j] is None else acc[j] + term
            for j in range(SUBS):
                at = jb * SUBS + j
                y_s[cg, rows(at), :] = acc[j] + gain * gs[j]
                qc_s[cg, rows(at), :] = (
                    wq[0] * qx[rows(at + 2), lanes]
                    + wq[1] * qx[rows(at + 1), lanes]
                    + wq[2] * qx[rows(at), lanes]
                )
        weights = spread(res, lanes)
        w_s[cg] = weights * jnp.exp(spread(rate, lanes) * (-(sub_f * steps + 1.0))[None])
        x = x_s[cg]
        x_s[cg] = jnp.where(sub_m >= 1, pltpu.roll(x, 1, 1), 0.0) * (weights * spread(a1, lanes))
        return carry

    def send_back(peer):
        return pltpu.make_async_remote_copy(
            src_ref=back.at[peer], dst_ref=inc.at[pl.ds(me * own, own)],
            send_sem=send_b.at[peer], recv_sem=recv_b.at[me],
            device_id={"ctx": peer}, device_id_type=MESH,
        )

    def arrive(owner):
        return pltpu.make_async_remote_copy(
            src_ref=back.at[owner], dst_ref=inc.at[pl.ds(owner * own, own)],
            send_sem=send_b.at[owner], recv_sem=recv_b.at[owner],
            device_id={"ctx": owner}, device_id_type=MESH,
        )

    lax.fori_loop(0, groups // 2, local, 0)

    def took(p, total):
        @pl.when(p != me)
        def _():
            pltpu.make_async_remote_copy(
                src_ref=ends.at[pl.ds(p * own, own)], dst_ref=got.at[p],
                send_sem=send_a.at[p], recv_sem=recv_a.at[p],
                device_id={"ctx": p}, device_id_type=MESH,
            ).wait_recv()

        back[p] = total

        @pl.when(p != me)
        def _():
            send_back(p).start()

        @pl.when(p == me)
        def _():
            inc[pl.ds(me * own, own)] = total

        return a256[pl.ds(me * own, own)] * total + got[p]

    lax.fori_loop(0, parts, took, jnp.zeros((own, SUBS, LANES), F32))

    lax.fori_loop(groups // 2, groups, local, 0)

    def finish(cg, carry):
        lanes = lanes_of(cg)
        for p in range(per_group):
            owner = cg * per_group + p

            @pl.when(owner != me)
            def _():
                arrive(owner).wait_recv()

        first = cg * (modes // SUBS)
        entry = jnp.stack(
            [
                jnp.broadcast_to(inc[first + n // SUBS, n % SUBS : n % SUBS + 1, :], (SUBS, LANES))
                for n in range(modes)
            ]
        )
        a = spread(a1, lanes)
        h = w_s[cg] * entry + x_s[cg]
        for j in range(0, steps, 2):
            pair = []
            for i in (j, j + 1):
                pair.append(qc_s[cg, rows(i), :] * (y_s[cg, rows(i), :] + tree_sum(h)))
                if i + 1 < steps:
                    h = a * h
            z_s[SUBS * j : SUBS * (j + 2), lanes] = jnp.concatenate(pair, axis=0).astype(BF16)
        return carry

    outs = []
    pieces = 4
    for s in range(pieces):
        lax.fori_loop(s * groups // pieces, (s + 1) * groups // pieces, finish, 0)
        width = channels // pieces
        for c in range(s * width, (s + 1) * width, 256):
            obuf[:, c : c + 256] = jnp.dot(
                perm[1], z_s[:, c : c + 256], preferred_element_type=F32
            ).astype(BF16)
        cols = pl.ds(s * width, width)
        c = pltpu.make_async_copy(obuf.at[:, cols], out_hbm.at[:, cols], out_sem.at[s])
        c.start()
        outs.append(c)

    @pl.when(me < parts - 1)
    def _():
        halo_copy.wait_send()

    def sent(p, carry):
        @pl.when(p != me)
        def _():
            send_ends(p).wait_send()
            send_back(p).wait_send()

        return carry

    lax.fori_loop(0, parts, sent, 0)
    for c in outs:
        c.wait()


def per_device(query_proj, key_proj, value_proj, short_weight, decay_rate, residue, skip_gain):
    parts = lax.axis_size("ctx")
    tokens, channels = query_proj.shape
    modes = decay_rate.shape[0]
    groups = channels // LANES
    steps = tokens // SUBS
    units = groups * modes // SUBS
    own = units // parts
    any_space = pl.BlockSpec(memory_space=pl.ANY)
    vm = pltpu.VMEM
    dma = pltpu.SemaphoreType.DMA
    return pl.pallas_call(
        functools.partial(layer_kernel, parts),
        out_shape=jax.ShapeDtypeStruct((tokens, channels), BF16),
        in_specs=[any_space] * 7,
        out_specs=any_space,
        scratch_shapes=[
            vm((tokens, channels), BF16),
            vm((tokens, channels), BF16),
            vm((tokens, channels), BF16),
            vm((3, 16, channels), BF16),
            vm(short_weight.shape, F32),
            vm(decay_rate.shape, F32),
            vm(residue.shape, F32),
            vm((1, channels), F32),
            vm((2, tokens, tokens), BF16),
            vm((tokens + 2 * SUBS, channels), F32),
            vm((tokens + 2 * SUBS, channels), F32),
            vm((tokens + 2 * SUBS, channels), F32),
            vm((SUBS, channels), F32),
            vm((SUBS, channels), F32),
            vm((modes, channels), F32),
            vm((modes, channels), F32),
            vm((modes, channels), F32),
            vm((modes, channels), F32),
            vm((units, SUBS, LANES), F32),
            vm((groups, steps, LANES), F32),
            vm((groups, tokens, LANES), F32),
            vm((groups, tokens, LANES), F32),
            vm((groups, modes, SUBS, LANES), F32),
            vm((groups, modes, SUBS, LANES), F32),
            vm((tokens, channels), BF16),
            vm((groups, tokens, LANES), F32),
            vm((units, SUBS, LANES), F32),
            vm((parts, own, SUBS, LANES), F32),
            vm((parts, own, SUBS, LANES), F32),
            vm((units, SUBS, LANES), F32),
            vm((tokens, channels), BF16),
            dma((3,)),
            dma((3,)),
            dma((4,)),
            dma((2,)),
            dma((parts,)),
            dma((parts,)),
            dma((parts,)),
            dma((parts,)),
            dma((4,)),
        ],
        compiler_params=pltpu.CompilerParams(
            collective_id=0, has_side_effects=True, vmem_limit_bytes=48 * 1024 * 1024
        ),
    )(
        query_proj, key_proj, value_proj, short_weight, decay_rate, residue,
        skip_gain.reshape(1, channels),
    )


def solution(mesh):
    rows = P(("group", "ctx"), None)
    return jax.shard_map(
        per_device,
        mesh=mesh,
        in_specs=(rows, rows, rows, P(), P(), P(), P()),
        out_specs=rows,
        check_vma=False,
    )
```

```python
import functools

import jax
import jax.numpy as jnp
from jax import lax
from jax.experimental import pallas as pl
from jax.experimental.pallas import tpu as pltpu
from jax.sharding import PartitionSpec as P

MESH = pl.DeviceIdType.MESH
F32 = jnp.float32
BF16 = jnp.bfloat16
LANES = 128
SUBS = 8


def tree_sum(x):
    while x.shape[0] > 1:
        half = x.shape[0] // 2
        x = x[:half] + x[half:]
    return x[0]


def layer_kernel(
    parts, q_hbm, k_hbm, v_hbm, sw_hbm, rate_hbm, res_hbm, skip_hbm, out_hbm,
    qbuf, kbuf, vbuf, sw, rate, res, skip,
    perm, qx, kx, vx, tail, halo,
    a1, a32, a64, a128, a256, inv1, inv2, resp, g_s, y_s, x_s, w_s, z_s, qc_s,
    ends, got, back, inc, obuf,
    load_sem, par_sem, halo_sem, send_a, recv_a, send_b, recv_b, out_sem,
):
    tokens, channels = qbuf.shape
    modes = rate.shape[0]
    groups = channels // LANES
    steps = tokens // SUBS
    units = groups * modes // SUBS
    own = units // parts
    per_group = modes // SUBS // own
    me = lax.axis_index("ctx")
    barrier = pltpu.get_barrier_semaphore()

    par_copies = []
    for i, (src, dst) in enumerate(((rate_hbm, rate), (res_hbm, res), (sw_hbm, sw), (skip_hbm, skip))):
        c = pltpu.make_async_copy(src, dst, par_sem.at[i])
        c.start()
        par_copies.append(c)
    loads = []
    for i, (src, dst) in enumerate(((k_hbm, kbuf), (v_hbm, vbuf), (q_hbm, qbuf))):
        c = pltpu.make_async_copy(src, dst, load_sem.at[i])
        c.start()
        loads.append(c)

    halo[...] = jnp.zeros(halo.shape, F32)

    def greet(i, carry):
        peer = lax.rem(me + i, parts)
        pl.semaphore_signal(barrier, inc=1, device_id={"ctx": peer}, device_id_type=MESH)
        return carry

    lax.fori_loop(1, parts, greet, 0)

    for c in par_copies:
        c.wait()
    negative = -rate[...]
    a1[...] = jnp.exp(negative)
    a32[...] = jnp.exp(negative * steps)
    a64[...] = jnp.exp(negative * (2 * steps))
    a128[...] = jnp.exp(negative * (4 * steps))
    for u in range(units):
        col = (u * SUBS // modes) * LANES
        row = (u * SUBS) % modes
        part = rate[row : row + SUBS, col : col + LANES]
        a256[u] = jnp.exp(part * (-float(tokens)))
        inv1[u] = jnp.exp(part)
        inv2[u] = jnp.exp(part * 2.0)

    row_id = lax.broadcasted_iota(jnp.int32, (tokens, tokens), 0)
    col_id = lax.broadcasted_iota(jnp.int32, (tokens, tokens), 1)
    perm[0] = jnp.where(col_id == (row_id % SUBS) * steps + row_id // SUBS, 1.0, 0.0).astype(BF16)
    perm[1] = jnp.where(row_id == (col_id % SUBS) * steps + col_id // SUBS, 1.0, 0.0).astype(BF16)

    sub_f = lax.broadcasted_iota(jnp.int32, (SUBS, LANES), 0).astype(F32)
    sub_w = lax.broadcasted_iota(jnp.int32, (SUBS, channels), 0)
    sub_m = lax.broadcasted_iota(jnp.int32, (modes, SUBS, LANES), 1)

    def lanes_of(cg):
        return pl.ds(pl.multiple_of(cg * LANES, LANES), LANES)

    def spread(ref, lanes):
        return jnp.stack([jnp.broadcast_to(ref[n : n + 1, lanes], (SUBS, LANES)) for n in range(modes)])

    def response(cg, carry):
        lanes = lanes_of(cg)
        rates = spread(rate, lanes)
        wave = spread(res, lanes) * jnp.exp(rates * (-sub_f)[None])
        eight = jnp.exp(rates * (-float(SUBS)))
        for b in range(steps // SUBS):
            resp[cg, SUBS * b : SUBS * b + SUBS, :] = tree_sum(wave)
            if b + 1 < steps // SUBS:
                wave = wave * eight
        return carry

    lax.fori_loop(0, groups, response, 0)

    def permuted(buf, dst):
        for c in range(0, channels, 256):
            dst[2 * SUBS :, c : c + 256] = jnp.dot(
                perm[0], buf[:, c : c + 256], preferred_element_type=F32
            )

    def margin(dst):
        for lag in (1, 2):
            last = dst[2 * SUBS + tokens - SUBS * lag : 2 * SUBS + tokens - SUBS * (lag - 1), :]
            dst[2 * SUBS - SUBS * lag : 2 * SUBS - SUBS * (lag - 1), :] = jnp.where(
                sub_w == 0, 0.0, pltpu.roll(last, 1, 0)
            )

    last_rows = [2 * SUBS + SUBS * (steps - lag) + SUBS - 1 for lag in (2, 1)]
    head_rows = [2 * SUBS, 3 * SUBS]

    for c, buf, dst in zip(loads, (kbuf, vbuf, qbuf), (kx, vx, qx)):
        c.wait()
        permuted(buf, dst)
        margin(dst)
    tail[...] = jnp.zeros(tail.shape, F32)
    for i, src in enumerate((kx, vx, qx)):
        for b, r in enumerate(last_rows):
            tail[2 * i + b : 2 * i + b + 1, :] = src[r : r + 1, :]

    def rows(j):
        return slice(SUBS * j, SUBS * j + SUBS)

    def tap(stream, lag, lanes):
        return jnp.broadcast_to(sw[stream, lag : lag + 1, lanes], (SUBS, LANES))

    def send_ends(owner):
        return pltpu.make_async_remote_copy(
            src_ref=ends.at[owner], dst_ref=got.at[me],
            send_sem=send_a.at[owner], recv_sem=recv_a.at[me],
            device_id={"ctx": owner}, device_id_type=MESH,
        )

    def gated_change(w, tails, heads):
        own_row, full = [], []
        for m in range(2):
            w0, w1, w2 = w[3 * m], w[3 * m + 1], w[3 * m + 2]
            before2, before1 = tails[2 * m], tails[2 * m + 1]
            x0, x1 = heads[2 * m], heads[2 * m + 1]
            zero = (w0 * x0, w0 * x1 + w1 * x0)
            own_row.append(zero)
            full.append((zero[0] + w1 * before1 + w2 * before2, zero[1] + w2 * before1))
        return [full[0][t] * full[1][t] - own_row[0][t] * own_row[1][t] for t in range(2)]

    def states(cg, carry):
        lanes = lanes_of(cg)
        a = spread(a1, lanes)
        wk = [tap(1, lag, lanes) for lag in range(3)]
        wv = [tap(2, lag, lanes) for lag in range(3)]
        k2, k1 = kx[rows(0), lanes], kx[rows(1), lanes]
        v2, v1 = vx[rows(0), lanes], vx[rows(1), lanes]
        h = None
        for j in range(steps):
            k0, v0 = kx[rows(j + 2), lanes], vx[rows(j + 2), lanes]
            g = (wk[0] * k0 + wk[1] * k1 + wk[2] * k2) * (wv[0] * v0 + wv[1] * v1 + wv[2] * v2)
            k2, k1, v2, v1 = k1, k0, v1, v0
            g_s[cg, rows(j), :] = g
            h = jnp.broadcast_to(g[None], (modes, SUBS, LANES)) if h is None else a * h + g[None]
        for lag, ref in ((1, a32), (2, a64), (4, a128)):
            factor = jnp.where(sub_m >= lag, spread(ref, lanes), 0.0)
            h = h + factor * pltpu.roll(h, lag, 1)
        x_s[cg] = h
        for p in range(per_group):
            owner = cg * per_group + p
            for n in range(own * SUBS):
                m = p * own * SUBS + n
                ends[owner, n // SUBS, n % SUBS : n % SUBS + 1, :] = h[m, SUBS - 1 : SUBS, :]
            line = 0
            for spots in (last_rows, head_rows):
                for src in (kx, vx):
                    for r in spots:
                        ends[owner, own, line : line + 1, :] = src[r : r + 1, lanes]
                        line += 1
        return carry

    lax.fori_loop(0, groups, states, 0)

    pl.semaphore_wait(barrier, parts - 1)
    halo_copy = pltpu.make_async_remote_copy(
        src_ref=tail, dst_ref=halo, send_sem=halo_sem.at[0], recv_sem=halo_sem.at[1],
        device_id={"ctx": lax.rem(me + 1, parts)}, device_id_type=MESH,
    )

    def send_all(i, carry):
        send_ends(lax.rem(me + i, parts)).start()
        return carry

    lax.fori_loop(1, parts, send_all, 0)
    got[me] = ends[me]

    @pl.when(me < parts - 1)
    def _():
        halo_copy.start()

    def local(cg, carry):
        lanes = lanes_of(cg)
        gain = jnp.broadcast_to(skip[0:1, lanes], (SUBS, LANES))
        wq = [tap(0, lag, lanes) for lag in range(3)]
        for jb in range(steps // SUBS):
            acc = [None] * SUBS
            for ib in range(jb + 1):
                gs = [g_s[cg, rows(ib * SUBS + i), :] for i in range(SUBS)]
                base = SUBS * (jb - ib)
                taps = {
                    d: jnp.broadcast_to(resp[cg, base + d : base + d + 1, :], (SUBS, LANES))
                    for d in range(1 - SUBS, SUBS)
                    if base + d >= 0
                }
                for i in range(SUBS):
                    for j in range(SUBS):
                        if j - i in taps:
                            term = taps[j - i] * gs[i]
                            acc[j] = term if acc[j] is None else acc[j] + term
            for j in range(SUBS):
                at = jb * SUBS + j
                y_s[cg, rows(at), :] = acc[j] + gain * gs[j]
                qc_s[cg, rows(at), :] = (
                    wq[0] * qx[rows(at + 2), lanes]
                    + wq[1] * qx[rows(at + 1), lanes]
                    + wq[2] * qx[rows(at), lanes]
                )
        weights = spread(res, lanes)
        w_s[cg] = weights * jnp.exp(spread(rate, lanes) * (-(sub_f * steps + 1.0))[None])
        x = x_s[cg]
        x_s[cg] = jnp.where(sub_m >= 1, pltpu.roll(x, 1, 1), 0.0) * (weights * spread(a1, lanes))
        return carry

    def send_back(peer):
        return pltpu.make_async_remote_copy(
            src_ref=back.at[peer], dst_ref=inc.at[pl.ds(me * own, own)],
            send_sem=send_b.at[peer], recv_sem=recv_b.at[me],
            device_id={"ctx": peer}, device_id_type=MESH,
        )

    def arrive(owner):
        return pltpu.make_async_remote_copy(
            src_ref=back.at[owner], dst_ref=inc.at[pl.ds(owner * own, own)],
            send_sem=send_b.at[owner], recv_sem=recv_b.at[owner],
            device_id={"ctx": owner}, device_id_type=MESH,
        )

    lax.fori_loop(0, groups * 3 // 4, local, 0)

    mine = pl.ds(me * own, own)
    own_lanes = lanes_of(me * own // (modes // SUBS))
    own_w = [sw[m, lag : lag + 1, own_lanes] for m in (1, 2) for lag in range(3)]

    def took(p, carry):
        total, before = carry

        @pl.when(p != me)
        def _():
            pltpu.make_async_remote_copy(
                src_ref=ends.at[p], dst_ref=got.at[p],
                send_sem=send_a.at[p], recv_sem=recv_a.at[p],
                device_id={"ctx": p}, device_id_type=MESH,
            ).wait_recv()

        extra = got[p, own]
        tails = [before[i : i + 1, :] for i in range(4)]
        heads = [extra[i : i + 1, :] for i in range(4, 8)]
        d0, d1 = gated_change(own_w, tails, heads)
        total = total + (inv1[mine] * d0[None] + inv2[mine] * d1[None])
        back[p] = total

        @pl.when(p != me)
        def _():
            send_back(p).start()

        @pl.when(p == me)
        def _():
            inc[mine] = total

        return a256[mine] * total + got[p, 0:own], extra

    lax.fori_loop(
        0, parts, took,
        (jnp.zeros((own, SUBS, LANES), F32), jnp.zeros((SUBS, LANES), F32)),
    )

    lax.fori_loop(groups * 3 // 4, groups, local, 0)

    @pl.when(me > 0)
    def _():
        halo_copy.wait_recv()

    def repair(cg, carry):
        lanes = lanes_of(cg)
        tails = [halo[i : i + 1, lanes] for i in range(6)]
        heads = [src[r : r + 1, lanes] for src in (kx, vx) for r in head_rows]
        w = [sw[m, lag : lag + 1, lanes] for m in (1, 2, 0) for lag in range(3)]
        d0, d1 = gated_change(w, tails, heads)
        gain = skip[0:1, lanes]
        early = jnp.sum(res[:, lanes] * jnp.exp(rate[:, lanes]), axis=0, keepdims=True)
        y_s[cg, 0:1, :] = y_s[cg, 0:1, :] + (gain * d0 - early * d1)
        y_s[cg, SUBS : SUBS + 1, :] = y_s[cg, SUBS : SUBS + 1, :] + gain * d1
        qc_s[cg, 0:1, :] = qc_s[cg, 0:1, :] + (w[7] * tails[5] + w[8] * tails[4])
        qc_s[cg, SUBS : SUBS + 1, :] = qc_s[cg, SUBS : SUBS + 1, :] + w[8] * tails[5]
        return carry

    lax.fori_loop(0, groups, repair, 0)

    def finish(cg, carry):
        lanes = lanes_of(cg)
        for p in range(per_group):
            owner = cg * per_group + p

            @pl.when(owner != me)
            def _():
                arrive(owner).wait_recv()

        first = cg * (modes // SUBS)
        entry = jnp.stack(
            [
                jnp.broadcast_to(inc[first + n // SUBS, n % SUBS : n % SUBS + 1, :], (SUBS, LANES))
                for n in range(modes)
            ]
        )
        a = spread(a1, lanes)
        h = w_s[cg] * entry + x_s[cg]
        for j in range(0, steps, 2):
            pair = []
            for i in (j, j + 1):
                pair.append(qc_s[cg, rows(i), :] * (y_s[cg, rows(i), :] + tree_sum(h)))
                if i + 1 < steps:
                    h = a * h
            z_s[SUBS * j : SUBS * (j + 2), lanes] = jnp.concatenate(pair, axis=0).astype(BF16)
        return carry

    outs = []
    pieces = 4
    for s in range(pieces):
        lax.fori_loop(s * groups // pieces, (s + 1) * groups // pieces, finish, 0)
        width = channels // pieces
        for c in range(s * width, (s + 1) * width, 256):
            obuf[:, c : c + 256] = jnp.dot(
                perm[1], z_s[:, c : c + 256], preferred_element_type=F32
            ).astype(BF16)
        cols = pl.ds(s * width, width)
        c = pltpu.make_async_copy(obuf.at[:, cols], out_hbm.at[:, cols], out_sem.at[s])
        c.start()
        outs.append(c)

    @pl.when(me < parts - 1)
    def _():
        halo_copy.wait_send()

    def sent(p, carry):
        @pl.when(p != me)
        def _():
            send_ends(p).wait_send()
            send_back(p).wait_send()

        return carry

    lax.fori_loop(0, parts, sent, 0)
    for c in outs:
        c.wait()


def per_device(query_proj, key_proj, value_proj, short_weight, decay_rate, residue, skip_gain):
    parts = lax.axis_size("ctx")
    tokens, channels = query_proj.shape
    modes = decay_rate.shape[0]
    groups = channels // LANES
    steps = tokens // SUBS
    units = groups * modes // SUBS
    own = units // parts
    any_space = pl.BlockSpec(memory_space=pltpu.HBM)
    vm = pltpu.VMEM
    dma = pltpu.SemaphoreType.DMA
    return pl.pallas_call(
        functools.partial(layer_kernel, parts),
        out_shape=jax.ShapeDtypeStruct((tokens, channels), BF16),
        in_specs=[any_space] * 7,
        out_specs=any_space,
        scratch_shapes=[
            vm((tokens, channels), BF16),
            vm((tokens, channels), BF16),
            vm((tokens, channels), BF16),
            vm(short_weight.shape, F32),
            vm(decay_rate.shape, F32),
            vm(residue.shape, F32),
            vm((1, channels), F32),
            vm((2, tokens, tokens), BF16),
            vm((tokens + 2 * SUBS, channels), F32),
            vm((tokens + 2 * SUBS, channels), F32),
            vm((tokens + 2 * SUBS, channels), F32),
            vm((SUBS, channels), F32),
            vm((SUBS, channels), F32),
            vm((modes, channels), F32),
            vm((modes, channels), F32),
            vm((modes, channels), F32),
            vm((modes, channels), F32),
            vm((units, SUBS, LANES), F32),
            vm((units, SUBS, LANES), F32),
            vm((units, SUBS, LANES), F32),
            vm((groups, steps, LANES), F32),
            vm((groups, tokens, LANES), F32),
            vm((groups, tokens, LANES), F32),
            vm((groups, modes, SUBS, LANES), F32),
            vm((groups, modes, SUBS, LANES), F32),
            vm((tokens, channels), BF16),
            vm((groups, tokens, LANES), F32),
            vm((parts, own + 1, SUBS, LANES), F32),
            vm((parts, own + 1, SUBS, LANES), F32),
            vm((parts, own, SUBS, LANES), F32),
            vm((units, SUBS, LANES), F32),
            vm((tokens, channels), BF16),
            dma((3,)),
            dma((4,)),
            dma((2,)),
            dma((parts,)),
            dma((parts,)),
            dma((parts,)),
            dma((parts,)),
            dma((4,)),
        ],
        compiler_params=pltpu.CompilerParams(
            collective_id=0, has_side_effects=True, vmem_limit_bytes=63 * 1024 * 1024
        ),
    )(
        query_proj, key_proj, value_proj, short_weight, decay_rate, residue,
        skip_gain.reshape(1, channels),
    )


def solution(mesh):
    rows = P(("group", "ctx"), None)
    return jax.shard_map(
        per_device,
        mesh=mesh,
        in_specs=(rows, rows, rows, P(), P(), P(), P()),
        out_specs=rows,
        check_vma=False,
    )
```

```python
import functools

import jax
import jax.numpy as jnp
from jax import lax
from jax.experimental import pallas as pl
from jax.experimental.pallas import tpu as pltpu
from jax.sharding import PartitionSpec as P

MESH = pl.DeviceIdType.MESH
F32 = jnp.float32
BF16 = jnp.bfloat16
LANES = 128
SUBS = 8


def tree_sum(x):
    while x.shape[0] > 1:
        half = x.shape[0] // 2
        x = x[:half] + x[half:]
    return x[0]


def layer_kernel(
    parts, q_hbm, k_hbm, v_hbm, sw_hbm, rate_hbm, res_hbm, skip_hbm, out_ref,
    qbuf, kbuf, vbuf, sw, rate, res, skip,
    perm, qx, kx, vx, tail, halo,
    a1, a32, a64, a128, a256, inv1, inv2, resp, g_s, y_s, x_s, w_s, qc_s,
    ends, got, back, inc,
    load_sem, par_sem, halo_sem, send_a, recv_a, send_b, recv_b,
):
    tokens, channels = qbuf.shape
    modes = rate.shape[0]
    groups = channels // LANES
    steps = tokens // SUBS
    units = groups * modes // SUBS
    own = units // parts
    per_group = modes // SUBS // own
    me = lax.axis_index("ctx")
    barrier = pltpu.get_barrier_semaphore()

    par_copies = []
    for i, (src, dst) in enumerate(((rate_hbm, rate), (res_hbm, res), (sw_hbm, sw), (skip_hbm, skip))):
        c = pltpu.make_async_copy(src, dst, par_sem.at[i])
        c.start()
        par_copies.append(c)
    loads = []
    for i, (src, dst) in enumerate(((k_hbm, kbuf), (v_hbm, vbuf), (q_hbm, qbuf))):
        c = pltpu.make_async_copy(src, dst, load_sem.at[i])
        c.start()
        loads.append(c)

    halo[...] = jnp.zeros(halo.shape, F32)

    def greet(i, carry):
        peer = lax.rem(me + i, parts)
        pl.semaphore_signal(barrier, inc=1, device_id={"ctx": peer}, device_id_type=MESH)
        return carry

    lax.fori_loop(1, parts, greet, 0)

    for c in par_copies:
        c.wait()
    negative = -rate[...]
    a1[...] = jnp.exp(negative)
    a32[...] = jnp.exp(negative * steps)
    a64[...] = jnp.exp(negative * (2 * steps))
    a128[...] = jnp.exp(negative * (4 * steps))
    for u in range(units):
        col = (u * SUBS // modes) * LANES
        row = (u * SUBS) % modes
        part = rate[row : row + SUBS, col : col + LANES]
        a256[u] = jnp.exp(part * (-float(tokens)))
        inv1[u] = jnp.exp(part)
        inv2[u] = jnp.exp(part * 2.0)

    row_id = lax.broadcasted_iota(jnp.int32, (tokens, tokens), 0)
    col_id = lax.broadcasted_iota(jnp.int32, (tokens, tokens), 1)
    perm[...] = jnp.where(col_id == (row_id % SUBS) * steps + row_id // SUBS, 1.0, 0.0).astype(BF16)

    sub_f = lax.broadcasted_iota(jnp.int32, (SUBS, LANES), 0).astype(F32)
    sub_w = lax.broadcasted_iota(jnp.int32, (SUBS, channels), 0)
    sub_m = lax.broadcasted_iota(jnp.int32, (modes, SUBS, LANES), 1)

    def lanes_of(cg):
        return pl.ds(pl.multiple_of(cg * LANES, LANES), LANES)

    def spread(ref, lanes):
        return jnp.stack([jnp.broadcast_to(ref[n : n + 1, lanes], (SUBS, LANES)) for n in range(modes)])

    def response(cg, carry):
        lanes = lanes_of(cg)
        rates = spread(rate, lanes)
        wave = spread(res, lanes) * jnp.exp(rates * (-sub_f)[None])
        eight = jnp.exp(rates * (-float(SUBS)))
        for b in range(steps // SUBS):
            resp[cg, SUBS * b : SUBS * b + SUBS, :] = tree_sum(wave)
            if b + 1 < steps // SUBS:
                wave = wave * eight
        return carry

    lax.fori_loop(0, groups, response, 0)

    def permuted(buf, dst):
        for c in range(0, channels, 256):
            dst[2 * SUBS :, c : c + 256] = jnp.dot(
                perm[...], buf[:, c : c + 256], preferred_element_type=F32
            )

    def margin(dst):
        for lag in (1, 2):
            last = dst[2 * SUBS + tokens - SUBS * lag : 2 * SUBS + tokens - SUBS * (lag - 1), :]
            dst[2 * SUBS - SUBS * lag : 2 * SUBS - SUBS * (lag - 1), :] = jnp.where(
                sub_w == 0, 0.0, pltpu.roll(last, 1, 0)
            )

    last_rows = [2 * SUBS + SUBS * (steps - lag) + SUBS - 1 for lag in (2, 1)]
    head_rows = [2 * SUBS, 3 * SUBS]

    for c, buf, dst in zip(loads, (kbuf, vbuf, qbuf), (kx, vx, qx)):
        c.wait()
        permuted(buf, dst)
        margin(dst)
    tail[...] = jnp.zeros(tail.shape, F32)
    for i, src in enumerate((kx, vx, qx)):
        for b, r in enumerate(last_rows):
            tail[2 * i + b : 2 * i + b + 1, :] = src[r : r + 1, :]

    def rows(j):
        return slice(SUBS * j, SUBS * j + SUBS)

    def tap(stream, lag, lanes):
        return jnp.broadcast_to(sw[stream, lag : lag + 1, lanes], (SUBS, LANES))

    def send_ends(owner):
        return pltpu.make_async_remote_copy(
            src_ref=ends.at[owner], dst_ref=got.at[me],
            send_sem=send_a.at[owner], recv_sem=recv_a.at[me],
            device_id={"ctx": owner}, device_id_type=MESH,
        )

    def gated_change(w, tails, heads):
        own_row, full = [], []
        for m in range(2):
            w0, w1, w2 = w[3 * m], w[3 * m + 1], w[3 * m + 2]
            before2, before1 = tails[2 * m], tails[2 * m + 1]
            x0, x1 = heads[2 * m], heads[2 * m + 1]
            zero = (w0 * x0, w0 * x1 + w1 * x0)
            own_row.append(zero)
            full.append((zero[0] + w1 * before1 + w2 * before2, zero[1] + w2 * before1))
        return [full[0][t] * full[1][t] - own_row[0][t] * own_row[1][t] for t in range(2)]

    def states(cg, carry):
        lanes = lanes_of(cg)
        a = spread(a1, lanes)
        wk = [tap(1, lag, lanes) for lag in range(3)]
        wv = [tap(2, lag, lanes) for lag in range(3)]
        k2, k1 = kx[rows(0), lanes], kx[rows(1), lanes]
        v2, v1 = vx[rows(0), lanes], vx[rows(1), lanes]
        h = None
        for j in range(steps):
            k0, v0 = kx[rows(j + 2), lanes], vx[rows(j + 2), lanes]
            g = (wk[0] * k0 + wk[1] * k1 + wk[2] * k2) * (wv[0] * v0 + wv[1] * v1 + wv[2] * v2)
            k2, k1, v2, v1 = k1, k0, v1, v0
            g_s[cg, rows(j), :] = g
            h = jnp.broadcast_to(g[None], (modes, SUBS, LANES)) if h is None else a * h + g[None]
        for lag, ref in ((1, a32), (2, a64), (4, a128)):
            factor = jnp.where(sub_m >= lag, spread(ref, lanes), 0.0)
            h = h + factor * pltpu.roll(h, lag, 1)
        x_s[cg] = h
        for p in range(per_group):
            owner = cg * per_group + p
            for n in range(own * SUBS):
                m = p * own * SUBS + n
                ends[owner, n // SUBS, n % SUBS : n % SUBS + 1, :] = h[m, SUBS - 1 : SUBS, :]
            line = 0
            for spots in (last_rows, head_rows):
                for src in (kx, vx):
                    for r in spots:
                        ends[owner, own, line : line + 1, :] = src[r : r + 1, lanes]
                        line += 1
        return carry

    lax.fori_loop(0, groups, states, 0)

    pl.semaphore_wait(barrier, parts - 1)
    halo_copy = pltpu.make_async_remote_copy(
        src_ref=tail, dst_ref=halo, send_sem=halo_sem.at[0], recv_sem=halo_sem.at[1],
        device_id={"ctx": lax.rem(me + 1, parts)}, device_id_type=MESH,
    )

    def send_all(i, carry):
        send_ends(lax.rem(me + i, parts)).start()
        return carry

    lax.fori_loop(1, parts, send_all, 0)
    got[me] = ends[me]

    @pl.when(me < parts - 1)
    def _():
        halo_copy.start()

    def local(cg, carry):
        lanes = lanes_of(cg)
        gain = jnp.broadcast_to(skip[0:1, lanes], (SUBS, LANES))
        wq = [tap(0, lag, lanes) for lag in range(3)]
        for jb in range(steps // SUBS):
            acc = [None] * SUBS
            for ib in range(jb + 1):
                gs = [g_s[cg, rows(ib * SUBS + i), :] for i in range(SUBS)]
                base = SUBS * (jb - ib)
                taps = {
                    d: jnp.broadcast_to(resp[cg, base + d : base + d + 1, :], (SUBS, LANES))
                    for d in range(1 - SUBS, SUBS)
                    if base + d >= 0
                }
                for i in range(SUBS):
                    for j in range(SUBS):
                        if j - i in taps:
                            term = taps[j - i] * gs[i]
                            acc[j] = term if acc[j] is None else acc[j] + term
            for j in range(SUBS):
                at = jb * SUBS + j
                y_s[cg, rows(at), :] = acc[j] + gain * gs[j]
                qc_s[cg, rows(at), :] = (
                    wq[0] * qx[rows(at + 2), lanes]
                    + wq[1] * qx[rows(at + 1), lanes]
                    + wq[2] * qx[rows(at), lanes]
                )
        weights = spread(res, lanes)
        w_s[cg] = weights * jnp.exp(spread(rate, lanes) * (-(sub_f * steps + 1.0))[None])
        x = x_s[cg]
        x_s[cg] = jnp.where(sub_m >= 1, pltpu.roll(x, 1, 1), 0.0) * (weights * spread(a1, lanes))
        return carry

    def send_back(peer):
        return pltpu.make_async_remote_copy(
            src_ref=back.at[peer], dst_ref=inc.at[pl.ds(me * own, own)],
            send_sem=send_b.at[peer], recv_sem=recv_b.at[me],
            device_id={"ctx": peer}, device_id_type=MESH,
        )

    def arrive(owner):
        return pltpu.make_async_remote_copy(
            src_ref=back.at[owner], dst_ref=inc.at[pl.ds(owner * own, own)],
            send_sem=send_b.at[owner], recv_sem=recv_b.at[owner],
            device_id={"ctx": owner}, device_id_type=MESH,
        )

    lax.fori_loop(0, groups * 3 // 4, local, 0)

    mine = pl.ds(me * own, own)
    own_lanes = lanes_of(me * own // (modes // SUBS))
    own_w = [sw[m, lag : lag + 1, own_lanes] for m in (1, 2) for lag in range(3)]

    def took(p, carry):
        total, before = carry

        @pl.when(p != me)
        def _():
            pltpu.make_async_remote_copy(
                src_ref=ends.at[p], dst_ref=got.at[p],
                send_sem=send_a.at[p], recv_sem=recv_a.at[p],
                device_id={"ctx": p}, device_id_type=MESH,
            ).wait_recv()

        extra = got[p, own]
        tails = [before[i : i + 1, :] for i in range(4)]
        heads = [extra[i : i + 1, :] for i in range(4, 8)]
        d0, d1 = gated_change(own_w, tails, heads)
        total = total + (inv1[mine] * d0[None] + inv2[mine] * d1[None])
        back[p] = total

        @pl.when(p != me)
        def _():
            send_back(p).start()

        @pl.when(p == me)
        def _():
            inc[mine] = total

        return a256[mine] * total + got[p, 0:own], extra

    lax.fori_loop(
        0, parts, took,
        (jnp.zeros((own, SUBS, LANES), F32), jnp.zeros((SUBS, LANES), F32)),
    )

    lax.fori_loop(groups * 3 // 4, groups, local, 0)

    @pl.when(me > 0)
    def _():
        halo_copy.wait_recv()

    def repair(cg, carry):
        lanes = lanes_of(cg)
        tails = [halo[i : i + 1, lanes] for i in range(6)]
        heads = [src[r : r + 1, lanes] for src in (kx, vx) for r in head_rows]
        w = [sw[m, lag : lag + 1, lanes] for m in (1, 2, 0) for lag in range(3)]
        d0, d1 = gated_change(w, tails, heads)
        gain = skip[0:1, lanes]
        early = jnp.sum(res[:, lanes] * jnp.exp(rate[:, lanes]), axis=0, keepdims=True)
        y_s[cg, 0:1, :] = y_s[cg, 0:1, :] + (gain * d0 - early * d1)
        y_s[cg, SUBS : SUBS + 1, :] = y_s[cg, SUBS : SUBS + 1, :] + gain * d1
        qc_s[cg, 0:1, :] = qc_s[cg, 0:1, :] + (w[7] * tails[5] + w[8] * tails[4])
        qc_s[cg, SUBS : SUBS + 1, :] = qc_s[cg, SUBS : SUBS + 1, :] + w[8] * tails[5]
        return carry

    lax.fori_loop(0, groups, repair, 0)

    def finish(cg, carry):
        lanes = lanes_of(cg)
        for p in range(per_group):
            owner = cg * per_group + p

            @pl.when(owner != me)
            def _():
                arrive(owner).wait_recv()

        first = cg * (modes // SUBS)
        entry = jnp.stack(
            [
                jnp.broadcast_to(inc[first + n // SUBS, n % SUBS : n % SUBS + 1, :], (SUBS, LANES))
                for n in range(modes)
            ]
        )
        a = spread(a1, lanes)
        h = w_s[cg] * entry + x_s[cg]
        for j in range(steps):
            g_s[cg, pl.ds(j, SUBS, stride=steps), :] = qc_s[cg, rows(j), :] * (
                y_s[cg, rows(j), :] + tree_sum(h)
            )
            if j + 1 < steps:
                h = a * h
        out_ref[:, lanes] = g_s[cg].astype(BF16)
        return carry

    lax.fori_loop(0, groups, finish, 0)

    @pl.when(me < parts - 1)
    def _():
        halo_copy.wait_send()

    def sent(p, carry):
        @pl.when(p != me)
        def _():
            send_ends(p).wait_send()
            send_back(p).wait_send()

        return carry

    lax.fori_loop(0, parts, sent, 0)


def per_device(query_proj, key_proj, value_proj, short_weight, decay_rate, residue, skip_gain):
    parts = lax.axis_size("ctx")
    tokens, channels = query_proj.shape
    modes = decay_rate.shape[0]
    groups = channels // LANES
    steps = tokens // SUBS
    units = groups * modes // SUBS
    own = units // parts
    any_space = pl.BlockSpec(memory_space=pltpu.HBM)
    vm = pltpu.VMEM
    dma = pltpu.SemaphoreType.DMA
    return pl.pallas_call(
        functools.partial(layer_kernel, parts),
        out_shape=pltpu.VMEM((tokens, channels), BF16),
        in_specs=[any_space] * 7,
        out_specs=pl.BlockSpec(memory_space=pltpu.VMEM),
        scratch_shapes=[
            vm((tokens, channels), BF16),
            vm((tokens, channels), BF16),
            vm((tokens, channels), BF16),
            vm(short_weight.shape, F32),
            vm(decay_rate.shape, F32),
            vm(residue.shape, F32),
            vm((1, channels), F32),
            vm((tokens, tokens), BF16),
            vm((tokens + 2 * SUBS, channels), F32),
            vm((tokens + 2 * SUBS, channels), F32),
            vm((tokens + 2 * SUBS, channels), F32),
            vm((SUBS, channels), F32),
            vm((SUBS, channels), F32),
            vm((modes, channels), F32),
            vm((modes, channels), F32),
            vm((modes, channels), F32),
            vm((modes, channels), F32),
            vm((units, SUBS, LANES), F32),
            vm((units, SUBS, LANES), F32),
            vm((units, SUBS, LANES), F32),
            vm((groups, steps, LANES), F32),
            vm((groups, tokens, LANES), F32),
            vm((groups, tokens, LANES), F32),
            vm((groups, modes, SUBS, LANES), F32),
            vm((groups, modes, SUBS, LANES), F32),
            vm((groups, tokens, LANES), F32),
            vm((parts, own + 1, SUBS, LANES), F32),
            vm((parts, own + 1, SUBS, LANES), F32),
            vm((parts, own, SUBS, LANES), F32),
            vm((units, SUBS, LANES), F32),
            dma((3,)),
            dma((4,)),
            dma((2,)),
            dma((parts,)),
            dma((parts,)),
            dma((parts,)),
            dma((parts,)),
        ],
        compiler_params=pltpu.CompilerParams(
            collective_id=0, has_side_effects=True, vmem_limit_bytes=62 * 1024 * 1024
        ),
    )(
        query_proj, key_proj, value_proj, short_weight, decay_rate, residue,
        skip_gain.reshape(1, channels),
    )


def solution(mesh):
    rows = P(("group", "ctx"), None)
    return jax.shard_map(
        per_device,
        mesh=mesh,
        in_specs=(rows, rows, rows, P(), P(), P(), P()),
        out_specs=rows,
        check_vma=False,
    )
```

```python
import functools

import jax
import jax.numpy as jnp
from jax import lax
from jax.experimental import pallas as pl
from jax.experimental.pallas import tpu as pltpu
from jax.sharding import PartitionSpec as P

MESH = pl.DeviceIdType.MESH
F32 = jnp.float32
BF16 = jnp.bfloat16
LANES = 128
SUBS = 8


def tree_sum(x):
    while x.shape[0] > 1:
        half = x.shape[0] // 2
        x = x[:half] + x[half:]
    return x[0]


def apart(a, b, count):
    total, place = 0, 1
    while place < count:
        total = total + place * lax.rem(lax.div(a, place) + lax.div(b, place), 2)
        place *= 2
    return total


def layer_kernel(
    parts, q_hbm, k_hbm, v_hbm, sw_hbm, rate_hbm, res_hbm, skip_hbm, out_ref,
    qbuf, kbuf, vbuf, sw, rate, res, skip,
    perm, qx, kx, vx, tail, halo,
    a1, a32, a64, a128, a256, inv1, inv2, resp, g_s, y_s, x_s, w_s, qc_s,
    ends, got, back, inc,
    load_sem, par_sem, halo_sem, send_a, recv_a, send_b, recv_b,
):
    tokens, channels = qbuf.shape
    modes = rate.shape[0]
    groups = channels // LANES
    steps = tokens // SUBS
    units = groups * modes // SUBS
    own = units // parts
    per_group = modes // SUBS // own
    me = lax.axis_index("ctx")
    barrier = pltpu.get_barrier_semaphore()

    par_copies = []
    for i, (src, dst) in enumerate(((rate_hbm, rate), (res_hbm, res), (sw_hbm, sw), (skip_hbm, skip))):
        c = pltpu.make_async_copy(src, dst, par_sem.at[i])
        c.start()
        par_copies.append(c)
    loads = []
    for i, (src, dst) in enumerate(((k_hbm, kbuf), (v_hbm, vbuf), (q_hbm, qbuf))):
        c = pltpu.make_async_copy(src, dst, load_sem.at[i])
        c.start()
        loads.append(c)

    halo[...] = jnp.zeros(halo.shape, F32)

    def greet(i, carry):
        peer = lax.rem(me + i, parts)
        pl.semaphore_signal(barrier, inc=1, device_id={"ctx": peer}, device_id_type=MESH)
        return carry

    lax.fori_loop(1, parts, greet, 0)

    for c in par_copies:
        c.wait()
    negative = -rate[...]
    a1[...] = jnp.exp(negative)
    a32[...] = jnp.exp(negative * steps)
    a64[...] = jnp.exp(negative * (2 * steps))
    a128[...] = jnp.exp(negative * (4 * steps))
    for u in range(units):
        col = (u * SUBS // modes) * LANES
        row = (u * SUBS) % modes
        part = rate[row : row + SUBS, col : col + LANES]
        a256[u] = jnp.exp(part * (-float(tokens)))
        inv1[u] = jnp.exp(part)
        inv2[u] = jnp.exp(part * 2.0)

    row_id = lax.broadcasted_iota(jnp.int32, (tokens, tokens), 0)
    col_id = lax.broadcasted_iota(jnp.int32, (tokens, tokens), 1)
    perm[...] = jnp.where(col_id == (row_id % SUBS) * steps + row_id // SUBS, 1.0, 0.0).astype(BF16)

    sub_f = lax.broadcasted_iota(jnp.int32, (SUBS, LANES), 0).astype(F32)
    sub_w = lax.broadcasted_iota(jnp.int32, (SUBS, channels), 0)
    sub_m = lax.broadcasted_iota(jnp.int32, (modes, SUBS, LANES), 1)

    def lanes_of(cg):
        return pl.ds(pl.multiple_of(cg * LANES, LANES), LANES)

    def spread(ref, lanes):
        return jnp.stack([jnp.broadcast_to(ref[n : n + 1, lanes], (SUBS, LANES)) for n in range(modes)])

    def response(cg, carry):
        lanes = lanes_of(cg)
        rates = spread(rate, lanes)
        wave = spread(res, lanes) * jnp.exp(rates * (-sub_f)[None])
        eight = jnp.exp(rates * (-float(SUBS)))
        for b in range(steps // SUBS):
            resp[cg, SUBS * b : SUBS * b + SUBS, :] = tree_sum(wave)
            if b + 1 < steps // SUBS:
                wave = wave * eight
        return carry

    lax.fori_loop(0, groups, response, 0)

    def permuted(buf, dst):
        for c in range(0, channels, 256):
            dst[2 * SUBS :, c : c + 256] = jnp.dot(
                perm[...], buf[:, c : c + 256], preferred_element_type=F32
            )

    def margin(dst):
        for lag in (1, 2):
            last = dst[2 * SUBS + tokens - SUBS * lag : 2 * SUBS + tokens - SUBS * (lag - 1), :]
            dst[2 * SUBS - SUBS * lag : 2 * SUBS - SUBS * (lag - 1), :] = jnp.where(
                sub_w == 0, 0.0, pltpu.roll(last, 1, 0)
            )

    last_rows = [2 * SUBS + SUBS * (steps - lag) + SUBS - 1 for lag in (2, 1)]
    head_rows = [2 * SUBS, 3 * SUBS]

    for c, buf, dst in zip(loads, (kbuf, vbuf, qbuf), (kx, vx, qx)):
        c.wait()
        permuted(buf, dst)
        margin(dst)
    tail[...] = jnp.zeros(tail.shape, F32)
    for i, src in enumerate((kx, vx, qx)):
        for b, r in enumerate(last_rows):
            tail[2 * i + b : 2 * i + b + 1, :] = src[r : r + 1, :]

    def rows(j):
        return slice(SUBS * j, SUBS * j + SUBS)

    def tap(stream, lag, lanes):
        return jnp.broadcast_to(sw[stream, lag : lag + 1, lanes], (SUBS, LANES))

    def send_ends(owner):
        return pltpu.make_async_remote_copy(
            src_ref=ends.at[owner], dst_ref=got.at[me],
            send_sem=send_a.at[owner], recv_sem=recv_a.at[me],
            device_id={"ctx": owner}, device_id_type=MESH,
        )

    def gated_change(w, tails, heads):
        own_row, full = [], []
        for m in range(2):
            w0, w1, w2 = w[3 * m], w[3 * m + 1], w[3 * m + 2]
            before2, before1 = tails[2 * m], tails[2 * m + 1]
            x0, x1 = heads[2 * m], heads[2 * m + 1]
            zero = (w0 * x0, w0 * x1 + w1 * x0)
            own_row.append(zero)
            full.append((zero[0] + w1 * before1 + w2 * before2, zero[1] + w2 * before1))
        return [full[0][t] * full[1][t] - own_row[0][t] * own_row[1][t] for t in range(2)]

    def states(cg, carry):
        lanes = lanes_of(cg)
        a = spread(a1, lanes)
        wk = [tap(1, lag, lanes) for lag in range(3)]
        wv = [tap(2, lag, lanes) for lag in range(3)]
        k2, k1 = kx[rows(0), lanes], kx[rows(1), lanes]
        v2, v1 = vx[rows(0), lanes], vx[rows(1), lanes]
        h = None
        for j in range(steps):
            k0, v0 = kx[rows(j + 2), lanes], vx[rows(j + 2), lanes]
            g = (wk[0] * k0 + wk[1] * k1 + wk[2] * k2) * (wv[0] * v0 + wv[1] * v1 + wv[2] * v2)
            k2, k1, v2, v1 = k1, k0, v1, v0
            g_s[cg, rows(j), :] = g
            h = jnp.broadcast_to(g[None], (modes, SUBS, LANES)) if h is None else a * h + g[None]
        for lag, ref in ((1, a32), (2, a64), (4, a128)):
            factor = jnp.where(sub_m >= lag, spread(ref, lanes), 0.0)
            h = h + factor * pltpu.roll(h, lag, 1)
        x_s[cg] = h
        for p in range(per_group):
            owner = cg * per_group + p
            for n in range(own * SUBS):
                m = p * own * SUBS + n
                ends[owner, n // SUBS, n % SUBS : n % SUBS + 1, :] = h[m, SUBS - 1 : SUBS, :]
            line = 0
            for spots in (last_rows, head_rows):
                for src in (kx, vx):
                    for r in spots:
                        ends[owner, own, line : line + 1, :] = src[r : r + 1, lanes]
                        line += 1
        return carry

    lax.fori_loop(0, groups, states, 0)

    pl.semaphore_wait(barrier, parts - 1)
    halo_copy = pltpu.make_async_remote_copy(
        src_ref=tail, dst_ref=halo, send_sem=halo_sem.at[0], recv_sem=halo_sem.at[1],
        device_id={"ctx": lax.rem(me + 1, parts)}, device_id_type=MESH,
    )

    def send_all(i, carry):
        send_ends(apart(me, parts - i, parts)).start()
        return carry

    lax.fori_loop(1, parts, send_all, 0)
    got[me] = ends[me]

    @pl.when(me < parts - 1)
    def _():
        halo_copy.start()

    def local(cg, carry):
        lanes = lanes_of(cg)
        gain = jnp.broadcast_to(skip[0:1, lanes], (SUBS, LANES))
        wq = [tap(0, lag, lanes) for lag in range(3)]
        for jb in range(steps // SUBS):
            acc = [None] * SUBS
            for ib in range(jb + 1):
                gs = [g_s[cg, rows(ib * SUBS + i), :] for i in range(SUBS)]
                base = SUBS * (jb - ib)
                taps = {
                    d: jnp.broadcast_to(resp[cg, base + d : base + d + 1, :], (SUBS, LANES))
                    for d in range(1 - SUBS, SUBS)
                    if base + d >= 0
                }
                for i in range(SUBS):
                    for j in range(SUBS):
                        if j - i in taps:
                            term = taps[j - i] * gs[i]
                            acc[j] = term if acc[j] is None else acc[j] + term
            for j in range(SUBS):
                at = jb * SUBS + j
                y_s[cg, rows(at), :] = acc[j] + gain * gs[j]
                qc_s[cg, rows(at), :] = (
                    wq[0] * qx[rows(at + 2), lanes]
                    + wq[1] * qx[rows(at + 1), lanes]
                    + wq[2] * qx[rows(at), lanes]
                )
        weights = spread(res, lanes)
        w_s[cg] = weights * jnp.exp(spread(rate, lanes) * (-(sub_f * steps + 1.0))[None])
        x = x_s[cg]
        x_s[cg] = jnp.where(sub_m >= 1, pltpu.roll(x, 1, 1), 0.0) * (weights * spread(a1, lanes))
        return carry

    def send_back(peer):
        return pltpu.make_async_remote_copy(
            src_ref=back.at[peer], dst_ref=inc.at[pl.ds(me * own, own)],
            send_sem=send_b.at[peer], recv_sem=recv_b.at[me],
            device_id={"ctx": peer}, device_id_type=MESH,
        )

    def arrive(owner):
        return pltpu.make_async_remote_copy(
            src_ref=back.at[owner], dst_ref=inc.at[pl.ds(owner * own, own)],
            send_sem=send_b.at[owner], recv_sem=recv_b.at[owner],
            device_id={"ctx": owner}, device_id_type=MESH,
        )

    lax.fori_loop(0, groups * 3 // 4, local, 0)

    mine = pl.ds(me * own, own)
    own_lanes = lanes_of(me * own // (modes // SUBS))
    own_w = [sw[m, lag : lag + 1, own_lanes] for m in (1, 2) for lag in range(3)]

    def took(p, carry):
        total, before = carry

        @pl.when(p != me)
        def _():
            pltpu.make_async_remote_copy(
                src_ref=ends.at[p], dst_ref=got.at[p],
                send_sem=send_a.at[p], recv_sem=recv_a.at[p],
                device_id={"ctx": p}, device_id_type=MESH,
            ).wait_recv()

        extra = got[p, own]
        tails = [before[i : i + 1, :] for i in range(4)]
        heads = [extra[i : i + 1, :] for i in range(4, 8)]
        d0, d1 = gated_change(own_w, tails, heads)
        total = total + (inv1[mine] * d0[None] + inv2[mine] * d1[None])
        back[p] = total

        @pl.when(p != me)
        def _():
            send_back(p).start()

        @pl.when(p == me)
        def _():
            inc[mine] = total

        return a256[mine] * total + got[p, 0:own], extra

    lax.fori_loop(
        0, parts, took,
        (jnp.zeros((own, SUBS, LANES), F32), jnp.zeros((SUBS, LANES), F32)),
    )

    lax.fori_loop(groups * 3 // 4, groups, local, 0)

    @pl.when(me > 0)
    def _():
        halo_copy.wait_recv()

    def repair(cg, carry):
        lanes = lanes_of(cg)
        tails = [halo[i : i + 1, lanes] for i in range(6)]
        heads = [src[r : r + 1, lanes] for src in (kx, vx) for r in head_rows]
        w = [sw[m, lag : lag + 1, lanes] for m in (1, 2, 0) for lag in range(3)]
        d0, d1 = gated_change(w, tails, heads)
        gain = skip[0:1, lanes]
        early = jnp.sum(res[:, lanes] * jnp.exp(rate[:, lanes]), axis=0, keepdims=True)
        y_s[cg, 0:1, :] = y_s[cg, 0:1, :] + (gain * d0 - early * d1)
        y_s[cg, SUBS : SUBS + 1, :] = y_s[cg, SUBS : SUBS + 1, :] + gain * d1
        qc_s[cg, 0:1, :] = qc_s[cg, 0:1, :] + (w[7] * tails[5] + w[8] * tails[4])
        qc_s[cg, SUBS : SUBS + 1, :] = qc_s[cg, SUBS : SUBS + 1, :] + w[8] * tails[5]
        return carry

    lax.fori_loop(0, groups, repair, 0)

    def finish(i, carry):
        cg = apart(me * own // (modes // SUBS), i, groups)
        lanes = lanes_of(cg)
        for p in range(per_group):
            owner = cg * per_group + p

            @pl.when(owner != me)
            def _():
                arrive(owner).wait_recv()

        first = cg * (modes // SUBS)
        entry = jnp.stack(
            [
                jnp.broadcast_to(inc[first + n // SUBS, n % SUBS : n % SUBS + 1, :], (SUBS, LANES))
                for n in range(modes)
            ]
        )
        a = spread(a1, lanes)
        h = w_s[cg] * entry + x_s[cg]
        for j in range(steps):
            g_s[cg, pl.ds(j, SUBS, stride=steps), :] = qc_s[cg, rows(j), :] * (
                y_s[cg, rows(j), :] + tree_sum(h)
            )
            if j + 1 < steps:
                h = a * h
        out_ref[:, lanes] = g_s[cg].astype(BF16)
        return carry

    lax.fori_loop(0, groups, finish, 0)

    @pl.when(me < parts - 1)
    def _():
        halo_copy.wait_send()

    def sent(p, carry):
        @pl.when(p != me)
        def _():
            send_ends(p).wait_send()
            send_back(p).wait_send()

        return carry

    lax.fori_loop(0, parts, sent, 0)


def per_device(query_proj, key_proj, value_proj, short_weight, decay_rate, residue, skip_gain):
    parts = lax.axis_size("ctx")
    tokens, channels = query_proj.shape
    modes = decay_rate.shape[0]
    groups = channels // LANES
    steps = tokens // SUBS
    units = groups * modes // SUBS
    own = units // parts
    any_space = pl.BlockSpec(memory_space=pltpu.HBM)
    vm = pltpu.VMEM
    dma = pltpu.SemaphoreType.DMA
    return pl.pallas_call(
        functools.partial(layer_kernel, parts),
        out_shape=pltpu.VMEM((tokens, channels), BF16),
        in_specs=[any_space] * 7,
        out_specs=pl.BlockSpec(memory_space=pltpu.VMEM),
        scratch_shapes=[
            vm((tokens, channels), BF16),
            vm((tokens, channels), BF16),
            vm((tokens, channels), BF16),
            vm(short_weight.shape, F32),
            vm(decay_rate.shape, F32),
            vm(residue.shape, F32),
            vm((1, channels), F32),
            vm((tokens, tokens), BF16),
            vm((tokens + 2 * SUBS, channels), F32),
            vm((tokens + 2 * SUBS, channels), F32),
            vm((tokens + 2 * SUBS, channels), F32),
            vm((SUBS, channels), F32),
            vm((SUBS, channels), F32),
            vm((modes, channels), F32),
            vm((modes, channels), F32),
            vm((modes, channels), F32),
            vm((modes, channels), F32),
            vm((units, SUBS, LANES), F32),
            vm((units, SUBS, LANES), F32),
            vm((units, SUBS, LANES), F32),
            vm((groups, steps, LANES), F32),
            vm((groups, tokens, LANES), F32),
            vm((groups, tokens, LANES), F32),
            vm((groups, modes, SUBS, LANES), F32),
            vm((groups, modes, SUBS, LANES), F32),
            vm((groups, tokens, LANES), F32),
            vm((parts, own + 1, SUBS, LANES), F32),
            vm((parts, own + 1, SUBS, LANES), F32),
            vm((parts, own, SUBS, LANES), F32),
            vm((units, SUBS, LANES), F32),
            dma((3,)),
            dma((4,)),
            dma((2,)),
            dma((parts,)),
            dma((parts,)),
            dma((parts,)),
            dma((parts,)),
        ],
        compiler_params=pltpu.CompilerParams(
            collective_id=0, has_side_effects=True, vmem_limit_bytes=62 * 1024 * 1024
        ),
    )(
        query_proj, key_proj, value_proj, short_weight, decay_rate, residue,
        skip_gain.reshape(1, channels),
    )


def solution(mesh):
    rows = P(("group", "ctx"), None)
    return jax.shard_map(
        per_device,
        mesh=mesh,
        in_specs=(rows, rows, rows, P(), P(), P(), P()),
        out_specs=rows,
        check_vma=False,
    )
```
